32 devices in a mesh: leaf: 8 (over z, y), sub: 4 (over x, core).
Axes of the slice: x: 2, y: 2, z: 4, core: 2. Of those that a mesh axis runs over, the one named last changes fastest.
Arguments:
- points: float32 [2048, 8, 128], P(('leaf', 'sub')), may hold values from -6 to 6
- probes: bfloat16 [2048, 32, 128], P(('leaf', 'sub')), may hold values from -6 to 6
- leaf_basis: bfloat16 [2048, 64, 128], P(('leaf', 'sub')), may hold values from -0.5 to 0.5
- mid_transfer: float32 [2048, 64, 64], P(('leaf', 'sub')), may hold values from -0.25 to 0.25
- top_transfer: float32 [256, 64, 64], P(('leaf', 'sub')), may hold values from -0.25 to 0.25
- mid_skeleton: float32 [256, 8, 64], P(('leaf', 'sub')), may hold values from -6 to 6
- top_skeleton: float32 [8, 8, 64], replicated, may hold values from -6 to 6
- near_list: int32 [2048, 8], P(('leaf', 'sub')), may hold values from -1 to 2047, as said below
- mid_list: int32 [256, 6], P(('leaf', 'sub')), may hold values from -1 to 255, as said below
- top_list: int32 [8, 6], P('leaf'), may hold values from -1 to 7, as said below
- inv_scale: float32 [8], replicated, may hold values from 0.15 to 0.5
- amplitude: float32 [1], replicated, may hold values from 0.03 to 0.1
- noise_var: float32 [1], replicated, may hold values from 0.2 to 1
Outputs:
- first_product: bfloat16 [2048, 32, 128], P(('leaf', 'sub'))
- second_product: bfloat16 [2048, 32, 128], P(('leaf', 'sub'))
The draws below stay inside these ranges and needn't reach their ends.
Inputs may be any that keep to these rules, and one draw needn't show every extreme that they name: `near_list`: entry 0 of row i is i; the other entries of a row are distinct leaves j != i with |j - i| <= 64, or -1. `mid_list`: the entries of a row m are distinct middle clusters j != m with |j - m| <= 8, or -1. `top_list`: the entries of a row t are distinct top clusters other than t, or -1.
All inputs are finite; a program needn't handle non-finite values.
Results may differ from the reference program's by a relative error of at most 0.0042.
Values may be sent and summed in bfloat16 or wider, within the bound.
No kernel may reach another device: no remote copies, remote signals or barrier semaphores. Data moves between devices by JAX's collectives and lax.ppermute only.
A program may use at most 128 MiB of HBM per device.

```python
import math
import jax
import jax.numpy as jnp
from jax import lax

LEAF = 128
R = 64
FEAT = 8
PROBES = 32
MID = 8
NEAR = 8
MID_NEAR = 6
TOP_NEAR = 6
LEAF_DEV = 64
MID_DEV = 8
NLEAF = 2048
NMID = 256
NTOP = 8


def pick_lists(key, rows, reach, count, keep_every):
    row_ids = jnp.arange(rows, dtype=jnp.int32)
    scores = jax.random.randint(key, (rows, 2 * reach), 0, 1048576)
    order = jnp.argsort(scores, axis=1, stable=True)[:, :count].astype(jnp.int32)
    offsets = jnp.where(order < reach, order - reach, order - reach + 1)
    targets = row_ids[:, None] + offsets
    keeping = jax.random.randint(jax.random.fold_in(key, 7), (rows, count), 0, 4) != 0
    keeping = keeping | (row_ids[:, None] % keep_every == 0)
    inside = (targets >= 0) & (targets < rows)
    return jnp.where(keeping & inside, targets, -1).astype(jnp.int32)


def draw_near_list(key, part):
    local_key = jax.random.fold_in(key, 101)
    others = pick_lists(local_key, NLEAF, LEAF_DEV, NEAR - 1, 5)
    selves = jnp.arange(NLEAF, dtype=jnp.int32)[:, None]
    return jnp.concatenate([selves, others], axis=1).astype(jnp.int32)


def draw_mid_list(key, part):
    local_key = jax.random.fold_in(key, 202)
    return pick_lists(local_key, NMID, MID_DEV, MID_NEAR, 3)


def draw_top_list(key, part):
    local_key = jax.random.fold_in(key, 303)
    row_ids = jnp.arange(NTOP, dtype=jnp.int32)
    scores = jax.random.randint(local_key, (NTOP, NTOP), 0, 1048576)
    scores = scores + (row_ids[:, None] == row_ids[None, :]).astype(jnp.int32) * 2097152
    order = jnp.argsort(scores, axis=1, stable=True)[:, :TOP_NEAR].astype(jnp.int32)
    keeping = jax.random.randint(jax.random.fold_in(local_key, 9), (NTOP, TOP_NEAR), 0, 4) != 0
    keeping = keeping | (row_ids[:, None] % 2 == 0)
    return jnp.where(keeping, order, -1).astype(jnp.int32)


def block_levels(rng, shape, pieces, low, largest):
    gain, own = 1.0, jax.random.fold_in(rng, 6)
    for dim, shards_of in pieces:
        steps = jnp.exp(jax.random.uniform(jax.random.fold_in(own, dim), (shards_of,), jnp.float32, low / len(pieces), largest / len(pieces)))
        gain = gain * jnp.repeat(steps, shape[dim] // shards_of).reshape([-1 if axis == dim else 1 for axis in range(len(shape))])
    return gain


def noise(rng, dims, width, most, split=(), kind=jnp.bfloat16):
    result = width * jax.random.normal(rng, dims, jnp.float32)
    if split:
        result = result * block_levels(rng, dims, split, -0.22, 0.18)
    return jnp.clip(result, -most, most).astype(kind)


def setup_inputs(seed: int = 0) -> dict:
    arg_keys = jax.random.split(jax.random.key(seed), 14)
    return {
        "points": noise(arg_keys[0], (NLEAF, FEAT, LEAF), 1.0, 6.0, ((0, 32),), jnp.float32),
        "probes": noise(arg_keys[1], (NLEAF, PROBES, LEAF), 1.0, 6.0, ((0, 32),)),
        "leaf_basis": noise(arg_keys[2], (NLEAF, R, LEAF), LEAF ** -0.5, 0.5, ((0, 32),)),
        "mid_transfer": noise(arg_keys[3], (NLEAF, R, R), (R * MID) ** -0.5, 0.25, ((0, 32),), jnp.float32),
        "top_transfer": noise(arg_keys[4], (NMID, R, R), (R * MID_DEV) ** -0.5, 0.25, ((0, 32),), jnp.float32),
        "mid_skeleton": noise(arg_keys[5], (NMID, FEAT, R), 1.0, 6.0, ((0, 32),), jnp.float32),
        "top_skeleton": noise(arg_keys[6], (NTOP, FEAT, R), 1.0, 6.0, (), jnp.float32),
        "near_list": draw_near_list(jax.random.fold_in(arg_keys[13], 71), 0),
        "mid_list": draw_mid_list(jax.random.fold_in(arg_keys[13], 71), 0),
        "top_list": draw_top_list(jax.random.fold_in(arg_keys[13], 71), 0),
        "inv_scale": jnp.clip(jnp.exp(jax.random.uniform(arg_keys[10], (FEAT,), jnp.float32, math.log(0.15), math.log(0.5))), 0.15, 0.5),
        "amplitude": jnp.clip(jnp.exp(jax.random.uniform(arg_keys[11], (1,), jnp.float32, math.log(0.03), math.log(0.1))), 0.03, 0.1),
        "noise_var": jnp.clip(jnp.exp(jax.random.uniform(arg_keys[12], (1,), jnp.float32, math.log(0.2), math.log(1.0))), 0.2, 1.0),
    }


def matern(left_side, right_side, inv_scale, amplitude):
    accumulated = None
    for feature in range(left_side.shape[-2]):
        difference = (left_side[..., feature, :, None] - right_side[..., feature, None, :]) * inv_scale[feature]
        if accumulated is None:
            accumulated = difference * difference
        else:
            accumulated = accumulated + difference * difference
    scaled = jnp.sqrt(3.0 * accumulated)
    return amplitude * (1.0 + scaled) * jnp.exp(-scaled)

def coupling(skeleton_own, skeleton_all, entries, inv_scale, amplitude):
    present = entries >= 0
    clipped = jnp.where(present, entries, 0)
    kernel_block = matern(skeleton_own[None], skeleton_all[clipped], inv_scale, amplitude)
    return kernel_block * present[:, None, None].astype(jnp.float32)

def near_part(points, vector, near_list, inv_scale, amplitude):

    def per_leaf(item):
        own_points, entries = item
        present = entries >= 0
        clipped = jnp.where(present, entries, 0)
        kernel_block = matern(own_points[None], points[clipped], inv_scale, amplitude)
        kernel_block = (kernel_block * present[:, None, None].astype(jnp.float32)).astype(jnp.bfloat16)
        gathered = vector[clipped]
        return jnp.einsum('knm,kpm->pn', kernel_block.astype(jnp.float32), gathered.astype(jnp.float32))
    return lax.map(per_leaf, (points, near_list))

def reference(points, probes, leaf_basis, mid_transfer, top_transfer, mid_skeleton, top_skeleton, near_list, mid_list, top_list, inv_scale, amplitude, noise_var):
    highest = lax.Precision.HIGHEST
    scale_amp = amplitude[0]
    mid_coupling = jax.vmap(lambda own, entries: coupling(own, mid_skeleton, entries, inv_scale, scale_amp))(mid_skeleton, mid_list)
    top_coupling = jax.vmap(lambda own, entries: coupling(own, top_skeleton, entries, inv_scale, scale_amp))(top_skeleton, top_list)
    mid_count = mid_skeleton.shape[0]
    top_count = top_skeleton.shape[0]
    mid_present = mid_list >= 0
    mid_clipped = jnp.where(mid_present, mid_list, 0)
    top_clipped = jnp.where(top_list >= 0, top_list, 0)
    transfer_groups = mid_transfer.reshape(mid_count, -1, R, R)

    def matvec(vector):
        leaf_coef = jnp.einsum('lpn,lrn->lpr', vector.astype(jnp.float32), leaf_basis.astype(jnp.float32))
        leaf_groups = leaf_coef.reshape(mid_count, -1, PROBES, R)
        mid_coef = jnp.einsum('mcpr,mcrs->mps', leaf_groups, transfer_groups, precision=highest)
        top_terms = jnp.einsum('mpr,mrs->mps', mid_coef, top_transfer, precision=highest)
        top_coef = lax.optimization_barrier(jnp.sum(top_terms.reshape(top_count, -1, PROBES, R), axis=1))
        mid_local = jnp.einsum('mkrs,mkps->mpr', mid_coupling, mid_coef[mid_clipped], precision=highest)
        top_local = jnp.einsum('tkrs,tkps->tpr', top_coupling, top_coef[top_clipped], precision=highest)
        top_down = jnp.repeat(top_local, mid_count // top_count, axis=0)
        mid_total = mid_local + jnp.einsum('mps,mrs->mpr', top_down, top_transfer, precision=highest)
        leaf_total = jnp.einsum('mps,mcrs->mcpr', mid_total, transfer_groups, precision=highest)
        leaf_total = leaf_total.reshape(-1, PROBES, R).astype(jnp.bfloat16)
        far = jnp.einsum('lpr,lrn->lpn', leaf_total.astype(jnp.float32), leaf_basis.astype(jnp.float32))
        near = near_part(points, vector, near_list, inv_scale, scale_amp)
        return (noise_var[0] * vector.astype(jnp.float32) + near + far).astype(jnp.bfloat16)
    first_product = matvec(probes)
    second_product = matvec(first_product)
    return (first_product, second_product)
```

```python
import functools
import math

import jax
import jax.numpy as jnp
from jax import lax
from jax.experimental import pallas as pl
from jax.experimental.pallas import tpu as pltpu
from jax.sharding import PartitionSpec as P

MATVECS = 2
AXES = ("leaf", "sub")
F32 = jnp.float32
BF16 = jnp.bfloat16
HIGHEST = lax.Precision.HIGHEST
LN2 = math.log(2.0)
DISTANCE_SCALE = math.sqrt(3.0) / LN2
MIB = 1 << 20

VMEM = pl.BlockSpec(memory_space=pltpu.VMEM)
SMEM = pl.BlockSpec(memory_space=pltpu.SMEM)


def split(value):
    high = value.astype(BF16).astype(F32)
    rest = value - high
    mid = rest.astype(BF16).astype(F32)
    low = (rest - mid).astype(BF16).astype(F32)
    return high, mid, low


def features(points, scale):
    scaled = points * scale
    high, mid, low = split(scaled)
    norm = jnp.sum(scaled * scaled, axis=0, keepdims=True)
    norm_high, norm_mid, norm_low = split(norm)
    row = lax.broadcasted_iota(jnp.int32, points.shape, 0)
    one = jnp.ones_like(norm)

    def rows(values):
        block = jnp.zeros_like(points)
        for index, value in enumerate(values):
            block = jnp.where(row == index, value, block)
        return block

    norms = (norm_high, norm_mid, norm_low)
    ones = (one, one, one)
    pad = jnp.zeros_like(points)
    left = jnp.concatenate([high, high, mid, mid, high, low, rows(norms + ones), pad], axis=0)
    right = jnp.concatenate(
        [-2.0 * x for x in (high, mid, high, mid, low, high)] + [rows(ones + norms), pad], axis=0
    )
    return left, right


def kernel_of(squared, amp):
    squared = jnp.maximum(squared, 1e-20)
    root = squared * lax.rsqrt(squared)
    return (amp + (amp * LN2) * root) * jnp.exp2(-root)


def dot(a, b, precision=None):
    return jnp.dot(a, b, preferred_element_type=F32, precision=precision)


def dot_nt(a, b):
    return lax.dot_general(a, b, (((1,), (1,)), ((), ())), preferred_element_type=F32)


def call(body, outs, in_specs, scratch=(), limit=24, cost=0, aliases=None, name=None, out_specs=None):
    return pl.pallas_call(
        body,
        out_shape=outs,
        in_specs=in_specs,
        out_specs=out_specs if out_specs is not None else [VMEM] * len(outs),
        scratch_shapes=list(scratch),
        input_output_aliases=aliases or {},
        compiler_params=pltpu.CompilerParams(vmem_limit_bytes=limit * MIB),
        cost_estimate=pl.CostEstimate(flops=cost, bytes_accessed=cost // 16, transcendentals=0),
        name=name,
    )


def near_items(order, slots, column, left, right, blocks, amp, start, count, group, near):
    def step(turn, carry):
        for inner in range(group):
            item = start + jnp.minimum(turn * group + inner, count - 1)
            slot = order[item]
            squared = dot(left[column(slots[slot])], right[lax.div(slot, near)])
            blocks[slot] = kernel_of(squared, amp).astype(BF16)
        return carry

    lax.fori_loop(0, lax.div(count + group - 1, group), step, 0)


def store_features(points, scale, left, right, base, count, unroll):
    def step(turn, carry):
        for inner in range(unroll):
            leaf = turn * unroll + inner
            left_block, right_block = features(points[leaf], scale)
            left[base + leaf] = left_block.T.astype(BF16)
            if right is not None:
                right[leaf] = right_block.astype(BF16)
        return carry

    lax.fori_loop(0, count // unroll, step, 0)


def local_body(near, order, slots, counts, amp, points, scale, blocks, right, left):
    leaves = points.shape[0]
    store_features(points, scale[...], left, right, 0, leaves, 4)
    near_items(
        order, slots, lambda j: j - leaves, left, right, blocks, amp[0], 0, counts[0], 4, near
    )


def halo_body(near, order, slots, counts, amp, low, high, scale, right, blocks_in, blocks, left):
    leaves = low.shape[0]
    store_features(low, scale[...], left, None, 0, leaves, 4)
    store_features(high, scale[...], left, None, leaves, leaves, 4)

    def column(j):
        return jnp.where(j < leaves, j, j - leaves)

    near_items(order, slots, column, left, right, blocks, amp[0], counts[0], counts[1], 4, near)
    empty = jnp.zeros(blocks.shape[1:], BF16)

    def clear(item, carry):
        blocks[order[item]] = empty
        return carry

    lax.fori_loop(counts[0] + counts[1], blocks.shape[0], clear, 0)


def up_group(vector, operator, group, members):
    total = None
    for member in range(members):
        leaf = group * members + member
        term = dot_nt(vector(leaf), operator[leaf])
        total = term if total is None else total + term
    rank = total.shape[1] // 2
    return total[:, :rank] + total[:, rank:]


def prepare_body(members, probes, basis, transfer, top_transfer, skeleton, operator, mid, top):
    rank = basis.shape[1]
    groups = mid.shape[0]
    probe_count = probes.shape[1]

    def step(group, total):
        for member in range(members):
            leaf = group * members + member
            matrix = transfer[leaf]
            high = matrix.astype(BF16)
            low = (matrix - high.astype(F32)).astype(BF16)
            both = jnp.concatenate([high.astype(F32), low.astype(F32)], axis=1).T.astype(BF16)
            product = dot(both, basis[leaf])
            folded = product[:rank] + product[rank:]
            upper = folded.astype(BF16)
            operator[leaf, :rank] = upper
            operator[leaf, rank:] = (folded - upper.astype(F32)).astype(BF16)
        coef = up_group(lambda leaf: probes[leaf], operator, group, members)
        mid[group, :probe_count] = coef
        mid[group, probe_count:] = skeleton[group]
        return total + dot(coef, top_transfer[group], HIGHEST)

    top[...] = lax.fori_loop(0, groups, step, jnp.zeros(top.shape, F32))


def skeleton_body(
    probe_count, entries, mid_ids, mid_on, top_ids, top_on, place, amp, own, low, high, tops, scale, mid_out, top_out, left, right
):
    groups = own.shape[0]
    scale = scale[...][:, : own.shape[2]]

    def store(source, base, keep_right):
        def step(group, carry):
            a, b = features(source[group, probe_count:], scale)
            left[base + group] = a.T.astype(BF16)
            if keep_right:
                right[group] = b.astype(BF16)
            return carry

        lax.fori_loop(0, groups, step, 0)

    store(low, 0, False)
    store(own, groups, True)
    store(high, 2 * groups, False)

    def mid_step(group, carry):
        for entry in range(entries):
            item = group * entries + entry
            value = kernel_of(dot(left[mid_ids[item]], right[group]), amp[0])
            mid_out[item] = jnp.where(mid_on[item] > 0, value, 0.0)
        return carry

    lax.fori_loop(0, groups, mid_step, 0)
    _, mine = features(tops[place[0]], scale)
    mine = mine.astype(BF16)
    for entry in range(top_out.shape[0]):
        other, _ = features(tops[top_ids[entry]], scale)
        value = kernel_of(dot(other.T.astype(BF16), mine), amp[0])
        top_out[entry] = jnp.where(top_on[entry] > 0, value, 0.0)


def middle_body(
    probe_count, entries, mid_ids, top_slots, own, low, high, tops, mid_coupling, top_coupling, top_transfer, total, table
):
    groups = own.shape[0]

    def fill(group, carry):
        table[group] = low[group, :probe_count]
        table[groups + group] = own[group, :probe_count]
        table[2 * groups + group] = high[group, :probe_count]
        return carry

    lax.fori_loop(0, groups, fill, 0)
    top_local = None
    for entry in range(top_coupling.shape[0]):
        term = dot(tops[top_slots[entry]], top_coupling[entry], HIGHEST)
        top_local = term if top_local is None else top_local + term

    def step(group, carry):
        value = lax.dot_general(
            top_local,
            top_transfer[group],
            (((1,), (1,)), ((), ())),
            preferred_element_type=F32,
            precision=HIGHEST,
        )
        for entry in range(entries):
            item = group * entries + entry
            value = value + dot(table[mid_ids[item]], mid_coupling[item], HIGHEST)
        total[group] = value
        return carry

    lax.fori_loop(0, groups, step, 0)


def product_body(members, near, again, slots, noise, low, own, high, blocks, operator, total, top_transfer, *rest):
    if again:
        out, mid, top, table = rest
    else:
        out, table = rest
    leaves, probe_count = own.shape[0], own.shape[1]
    rank = total.shape[2]
    points = own.shape[2]

    def fill(leaf, carry):
        table[leaf] = low[leaf]
        table[leaves + leaf] = own[leaf]
        table[2 * leaves + leaf] = high[leaf]
        return carry

    lax.fori_loop(0, leaves, fill, 0, unroll=4)

    def step(group, carry):
        local = total[group]
        upper = local.astype(BF16)
        lower = (local - upper.astype(F32)).astype(BF16)
        twice = jnp.concatenate([upper, upper], axis=1)
        for member in range(members):
            leaf = group * members + member
            gathered = jnp.concatenate(
                [table[slots[leaf * near + entry]] for entry in range(near)], axis=1
            )
            weights = blocks[pl.ds(leaf * near, near)].reshape(near * points, points)
            value = dot(gathered, weights)
            value = value + dot(twice, operator[leaf]) + dot(lower, operator[leaf, :rank])
            value = value + noise[0] * own[leaf].astype(F32)
            out[leaf] = value.astype(BF16)
        if again:
            coef = up_group(lambda leaf: out[leaf], operator, group, members)
            mid[group] = coef
            carry = carry + dot(coef, top_transfer[group], HIGHEST)
        return carry

    groups = total.shape[0]
    result = lax.fori_loop(0, groups, step, jnp.zeros((probe_count, rank), F32))
    if again:
        top[...] = result


def neighbours(block):
    count = lax.axis_size(AXES)
    forward = [(i, i + 1) for i in range(count - 1)]
    backward = [(target, source) for source, target in forward]
    return lax.ppermute(block, AXES, forward), lax.ppermute(block, AXES, backward)


def top_exchange(partial):
    size = lax.axis_size("sub")
    step = 1
    while step < size:
        partial = partial + lax.ppermute(partial, "sub", [(i, i ^ step) for i in range(size)])
        step *= 2
    blocks = partial[None]
    size = lax.axis_size("leaf")
    step = 1
    while step < size:
        other = lax.ppermute(blocks, "leaf", [(i, i ^ step) for i in range(size)])
        blocks = jnp.concatenate([blocks, other], axis=0)
        step *= 2
    return blocks


def work_list(kind):
    count = kind.shape[0]
    item = jnp.arange(count, dtype=jnp.int32)
    before = (kind[:, None] > kind[None, :]) | (
        (kind[:, None] == kind[None, :]) & (item[:, None] > item[None, :])
    )
    place = jnp.sum(before.astype(jnp.int32), axis=1)
    order = jnp.sum(jnp.where(place[:, None] == item[None, :], item[:, None], 0), axis=0)
    counts = jnp.stack([jnp.sum((kind == which).astype(jnp.int32)) for which in range(2)])
    return order, counts


def on_device(
    points,
    probes,
    leaf_basis,
    mid_transfer,
    top_transfer,
    mid_skeleton,
    top_skeleton,
    near_list,
    mid_list,
    top_list,
    inv_scale,
    amplitude,
    noise_var,
):
    leaves, feat, size = points.shape
    groups, _, rank = mid_skeleton.shape
    probe_count = probes.shape[1]
    members = leaves // groups
    near = near_list.shape[1]
    entries = mid_list.shape[1]
    position = lax.axis_index("leaf") * lax.axis_size("sub") + lax.axis_index("sub")
    top_index = lax.axis_index("leaf")

    low_points, high_points = neighbours(points)
    low_probes, high_probes = neighbours(probes)

    flat = near_list.reshape(-1)
    present = flat >= 0
    slots = jnp.where(present, flat - position * leaves + leaves, leaves)
    outside = (slots < leaves) | (slots >= 2 * leaves)
    kind = jnp.where(present, outside.astype(jnp.int32), 2)
    order, counts = work_list(kind)
    scale = jnp.broadcast_to((inv_scale * DISTANCE_SCALE)[:, None], (feat, size))

    mid_flat = mid_list.reshape(-1)
    mid_on = (mid_flat >= 0).astype(jnp.int32)
    mid_ids = jnp.where(mid_flat >= 0, mid_flat - position * groups + groups, groups)
    top_row = top_list.reshape(-1)
    top_on = (top_row >= 0).astype(jnp.int32)
    top_ids = jnp.where(top_row >= 0, top_row, 0)
    top_slots = jnp.where(top_row >= 0, top_row ^ top_index, 0)
    place = top_index.reshape(1).astype(jnp.int32)

    sds = jax.ShapeDtypeStruct
    operator, mid, top = call(
        functools.partial(prepare_body, members),
        [
            sds((leaves, 2 * rank, size), BF16),
            sds((groups, probe_count + feat, rank), F32),
            sds((probe_count, rank), F32),
        ],
        [VMEM] * 5,
        name="prepare",
        cost=2 * leaves * rank * rank * size * 2,
    )(probes, leaf_basis, mid_transfer, top_transfer, mid_skeleton)

    blocks, right = call(
        functools.partial(local_body, near),
        [sds((leaves * near, size, size), BF16), sds((leaves, 8 * feat, size), BF16)],
        [SMEM] * 4 + [VMEM] * 2,
        scratch=[pltpu.VMEM((leaves, size, 8 * feat), BF16)],
        name="near_local",
        cost=leaves * near * size * size * 40,
    )(order, slots, counts, amplitude, points, scale)

    blocks = call(
        functools.partial(halo_body, near),
        [sds((leaves * near, size, size), BF16)],
        [SMEM] * 4 + [VMEM] * 5,
        scratch=[pltpu.VMEM((2 * leaves, size, 8 * feat), BF16)],
        aliases={8: 0},
        name="near_halo",
        cost=leaves * near * size * size * 40,
    )(order, slots, counts, amplitude, low_points, high_points, scale, right, blocks)[0]

    mid_coupling = top_coupling = None
    vector, low, high = probes, low_probes, high_probes
    results = []
    for turn in range(MATVECS):
        if turn > 0:
            low, high = neighbours(vector)
        low_mid, high_mid = neighbours(mid)
        tops = top_exchange(top)
        if turn == 0:
            mid_coupling, top_coupling = call(
                functools.partial(skeleton_body, probe_count, entries),
                [
                    sds((groups * entries, rank, rank), F32),
                    sds((top_row.shape[0], rank, rank), F32),
                ],
                [SMEM] * 6 + [VMEM] * 5,
                scratch=[
                    pltpu.VMEM((3 * groups, rank, 8 * feat), BF16),
                    pltpu.VMEM((groups, 8 * feat, rank), BF16),
                ],
                name="skeleton",
                cost=groups * entries * rank * rank * 40,
            )(
                mid_ids, mid_on, top_ids, top_on, place, amplitude,
                mid, low_mid, high_mid, top_skeleton, scale,
            )
        total = call(
            functools.partial(middle_body, probe_count, entries),
            [sds((groups, probe_count, rank), F32)],
            [SMEM] * 2 + [VMEM] * 7,
            scratch=[pltpu.VMEM((3 * groups, probe_count, rank), F32)],
            name="middle",
            cost=groups * entries * rank * rank * probe_count * 12,
        )(
            mid_ids, top_slots, mid, low_mid, high_mid, tops,
            mid_coupling, top_coupling, top_transfer,
        )[0]
        again = turn + 1 < MATVECS
        outs = [sds(vector.shape, BF16)]
        if again:
            outs += [sds((groups, probe_count, rank), F32), sds((probe_count, rank), F32)]
        values = call(
            functools.partial(product_body, members, near, again),
            outs,
            [SMEM] * 2 + [VMEM] * 7,
            scratch=[pltpu.VMEM((3 * leaves, probe_count, size), BF16)],
            name="product",
            cost=2 * leaves * near * size * size * probe_count,
        )(slots, noise_var, low, vector, high, blocks, operator, total, top_transfer)
        vector = values[0]
        results.append(vector)
        if again:
            mid, top = values[1], values[2]
    return (results[0], results[1])


def solution(mesh):
    whole = P(AXES, None, None)
    in_specs = (
        whole, whole, whole, whole, whole, whole,
        P(), P(AXES, None), P(AXES, None), P("leaf", None), P(), P(), P(),
    )
    return jax.shard_map(
        on_device, mesh=mesh, in_specs=in_specs, out_specs=(whole, whole), check_vma=False
    )
```

```python
import functools
import math

import jax
import jax.numpy as jnp
from jax import lax
from jax.experimental import pallas as pl
from jax.experimental.pallas import tpu as pltpu
from jax.sharding import PartitionSpec as P


MATVECS = 2
AXES = ("leaf", "sub")
F32 = jnp.float32
BF16 = jnp.bfloat16
LN2 = math.log(2.0)
DISTANCE_SCALE = math.sqrt(3.0) / LN2
MIB = 1 << 20
GROUP = 16
PARTS = 4

VMEM = pl.BlockSpec(memory_space=pltpu.VMEM)
SMEM = pl.BlockSpec(memory_space=pltpu.SMEM)
HBM = pl.BlockSpec(memory_space=pltpu.HBM)


def split(value):
    high = value.astype(BF16).astype(F32)
    rest = value - high
    mid = rest.astype(BF16).astype(F32)
    low = (rest - mid).astype(BF16).astype(F32)
    return high, mid, low


def features(terms):
    high, mid, low = terms
    pad = jnp.zeros_like(high)
    low = pad if low is None else low
    scaled = high + mid + low
    norm = jnp.sum(scaled * scaled, axis=0, keepdims=True)
    norm_high, norm_mid, norm_low = split(norm)
    row = lax.broadcasted_iota(jnp.int32, high.shape, 0)
    one = jnp.ones_like(norm)

    def rows(values):
        block = pad
        for index, value in enumerate(values):
            block = jnp.where(row == index, value, block)
        return block

    norms = (norm_high, norm_mid, norm_low)
    ones = (one, one, one)
    left = jnp.concatenate([high, high, mid, mid, high, low, rows(norms + ones), pad], axis=0)
    right = jnp.concatenate(
        [-2.0 * x for x in (high, mid, high, mid, low, high)] + [rows(ones + norms), pad], axis=0
    )
    return left, right


def kernel_of(squared, amp):
    squared = jnp.maximum(squared, 1e-20)
    root = squared * lax.rsqrt(squared)
    return (amp + (amp * LN2) * root) * jnp.exp2(-root)


def dot(a, b):
    return jnp.dot(a, b, preferred_element_type=F32)


def dot_nt(a, b):
    return lax.dot_general(a, b, (((1,), (1,)), ((), ())), preferred_element_type=F32)


def call(body, outs, in_specs, scratch=(), limit=24 * MIB, micros=1, aliases=None, out_specs=None):
    return pl.pallas_call(
        body,
        out_shape=outs,
        in_specs=in_specs,
        out_specs=out_specs if out_specs is not None else [VMEM] * len(outs),
        scratch_shapes=list(scratch),
        input_output_aliases=aliases or {},
        compiler_params=pltpu.CompilerParams(vmem_limit_bytes=limit),
        cost_estimate=pl.CostEstimate(
            flops=int(micros * 1.1e9), bytes_accessed=int(micros * 1e6), transcendentals=0
        ),
    )


def decode(items, item, near):
    code = items[item]
    slot = code & 0xFFFF
    return slot, lax.shift_right_logical(slot, near.bit_length() - 1), lax.shift_right_logical(code, 16)


def near_items(items, left, right, blocks, amp, start, count, near, part=0, parts=1):
    turns = lax.div(count + GROUP - 1, GROUP)

    def step(turn, carry):
        for inner in range(GROUP):
            item = start + jnp.minimum(turn * GROUP + inner, count - 1)
            slot, row, column = decode(items, item, near)
            blocks[slot] = kernel_of(dot(left[column], right[row]), amp).astype(BF16)
        return carry

    lax.fori_loop(lax.div(turns * part, parts), lax.div(turns * (part + 1), parts), step, 0)


def scale_block(inv_scale, shape):
    row = lax.broadcasted_iota(jnp.int32, shape, 0)
    block = jnp.zeros(shape, F32)
    for feature in range(shape[0]):
        block = jnp.where(row == feature, inv_scale[feature] * DISTANCE_SCALE, block)
    return block


def local_body(near, part, parts, items, amp, inv_scale, *refs):
    slots = items.shape[0] - 2
    if part == 0:
        points, blocks, right, left = refs
        leaves, feat, size = points.shape
        scale = scale_block(inv_scale, (feat, size))

        def step(turn, carry):
            for inner in range(8):
                leaf = turn * 8 + inner
                left_block, right_block = features(split(points[leaf] * scale))
                left[leaf] = left_block.T.astype(BF16)
                right[leaf] = right_block.astype(BF16)
            return carry

        lax.fori_loop(0, leaves // 8, step, 0)
    else:
        right, left, _, blocks = refs
    near_items(
        items, left, right, blocks, amp[0], 0, items[slots], near, part, parts
    )


def halo_body(near, items, amp, low, high, right, blocks_in, blocks, left):
    leaves, _, _ = right.shape
    feat = right.shape[1] // 8
    slots = items.shape[0] - 2

    def step(turn, carry):
        for inner in range(4):
            leaf = turn * 4 + inner
            for base, source in ((0, low), (leaves, high)):
                terms = source[leaf, : 2 * feat].astype(F32)
                left_block, _ = features((terms[:feat], terms[feat:], None))
                left[base + leaf] = left_block.T.astype(BF16)
        return carry

    lax.fori_loop(0, leaves // 4, step, 0)
    near_items(
        items, left, right, blocks, amp[0], items[slots], items[slots + 1], near
    )
    empty = jnp.zeros(blocks.shape[1:], BF16)

    def clear(item, carry):
        blocks[decode(items, item, near)[0]] = empty
        return carry

    lax.fori_loop(items[slots] + items[slots + 1], slots, clear, 0)


def pair(value, axis):
    upper = value.astype(BF16)
    lower = (value - upper.astype(F32)).astype(BF16)
    return jnp.concatenate([upper, lower], axis=axis)


def quarters(product):
    rows, columns = product.shape[0] // 2, product.shape[1] // 2
    product = product[:rows] + product[rows:]
    return product[:, :columns] + product[:, columns:]


def up_group(vector, operator, group, members):
    total = None
    for member in range(members):
        leaf = group * members + member
        term = dot_nt(vector(leaf), operator[leaf])
        total = term if total is None else total + term
    rank = total.shape[1] // 2
    return total[:, :rank] + total[:, rank:]


def up_top(coef, matrix):
    both = pair(coef, 0)
    product = dot(jnp.concatenate([both, both], axis=1), matrix)
    rows = coef.shape[0]
    return product[:rows] + product[rows:]


def prepare_body(
    members, inv_scale, points_at, probes_at, basis_at, transfer_at, top_transfer_at, skeleton_at,
    operator, packed, top, top_split,
    points, basis, transfer, top_transfer, skeleton, sems, more_sems,
):
    leaves, feat, size = points.shape
    rank = basis.shape[1]
    groups = top_split.shape[0]
    skip = 2 * feat
    scale = scale_block(inv_scale, (feat, size))

    def copies(group):
        where = pl.ds(group * members, members)
        pairs = (
            (probes_at.at[where], packed.at[where, skip:, :]),
            (basis_at.at[where], basis.at[where]),
            (transfer_at.at[where], transfer.at[where]),
        )
        return [
            pltpu.make_async_copy(source, target, sems.at[index, group])
            for index, (source, target) in enumerate(pairs)
        ]

    pairs = ((points_at, points), (skeleton_at, skeleton), (top_transfer_at, top_transfer))
    whole = [
        pltpu.make_async_copy(source, target, more_sems.at[index])
        for index, (source, target) in enumerate(pairs)
    ]
    for copy in whole:
        copy.start()
    for group in range(groups):
        for copy in copies(group):
            copy.start()
    for copy in whole:
        copy.wait()

    def step(group, total):
        for copy in copies(group):
            copy.wait()
        for member in range(members):
            leaf = group * members + member
            both = pair(transfer[leaf], 1).T
            product = dot(both, basis[leaf])
            operator[leaf] = pair(product[:rank] + product[rank:], 0)
            high, mid, _ = split(points[leaf] * scale)
            packed[leaf, :skip] = jnp.concatenate([high, mid], axis=0).astype(BF16)
        coef = up_group(lambda leaf: packed[leaf, skip:], operator, group, members)
        packed[leaves + group, skip:] = pair(coef, 1)
        high, mid, low = split(skeleton[group] * scale[:, :rank])
        packed[leaves + group, :skip, :rank] = jnp.concatenate([high, mid], axis=0).astype(BF16)
        packed[leaves + group, :skip, rank:] = jnp.concatenate([low, low], axis=0).astype(BF16)
        matrix = pair(top_transfer[group], 0)
        top_split[group] = matrix
        return total + up_top(coef, matrix)

    top[...] = lax.fori_loop(0, groups, step, jnp.zeros(top.shape, F32))


def skeleton_body(
    entries, mid_list, top_list, amp, inv_scale, own, low, high, tops, mid_out, top_out, left, right
):
    groups = right.shape[0]
    leaves = own.shape[0] - groups
    feat, rank = tops.shape[1:]
    scale = scale_block(inv_scale, (feat, rank))
    first = (lax.axis_index("leaf") * lax.axis_size("sub") + lax.axis_index("sub") - 1) * groups

    def step(turn, carry):
        for inner in range(2):
            group = turn * 2 + inner
            for place, source in enumerate((low, own, high)):
                terms = source[leaves + group, : 2 * feat].astype(F32)
                a, b = features((terms[:feat, :rank], terms[feat:, :rank], terms[:feat, rank:]))
                left[place * groups + group] = a.T.astype(BF16)
                if place == 1:
                    right[group] = b.astype(BF16)
        return carry

    lax.fori_loop(0, groups // 2, step, 0)

    def mid_step(group, carry):
        for entry in range(entries):
            index = mid_list[group, entry]
            place = jnp.where(index >= 0, index - first, groups)
            value = kernel_of(dot(left[place], right[group]), amp[0])
            value = value * jnp.where(index >= 0, 1.0, 0.0)
            mid_out[group * entries + entry] = pair(value, 1)
        return carry

    lax.fori_loop(0, groups, mid_step, 0)
    _, mine = features(split(tops[lax.axis_index("leaf")] * scale))
    mine = mine.astype(BF16)
    for entry in range(top_out.shape[0]):
        index = top_list[0, entry]
        other, _ = features(split(tops[jnp.maximum(index, 0)] * scale))
        value = kernel_of(dot(other.T.astype(BF16), mine), amp[0])
        top_out[entry] = pair(value * jnp.where(index >= 0, 1.0, 0.0), 1)


def middle_body(
    entries, summed, mid_list, top_list, own, low, high, tops, mid_coupling, top_coupling, top_split,
    total, table,
):
    groups, probe_count = total.shape[0], total.shape[1]
    rank = total.shape[2]
    shares = lax.axis_size("sub")
    first = (lax.axis_index("leaf") * shares + lax.axis_index("sub") - 1) * groups

    skip = own.shape[1] - probe_count

    def fill(group, carry):
        for place, source in enumerate((low, own, high)):
            both = source[source.shape[0] - groups + group, skip:]
            table[place * groups + group, :probe_count] = both[:, :rank]
            table[place * groups + group, probe_count:] = both[:, rank:]
        return carry

    lax.fori_loop(0, groups, fill, 0, unroll=2)
    product = None
    for entry in range(top_coupling.shape[0]):
        index = top_list[0, entry]
        if summed:
            coef = tops[jnp.where(index >= 0, index ^ lax.axis_index("leaf"), 0)]
        else:
            where = jnp.maximum(index, 0) * shares
            coef = tops[where].astype(F32)
            for share in range(1, shares):
                coef = coef + tops[where + share].astype(F32)
            coef = coef[:, :rank] + coef[:, rank:]
        term = dot(pair(coef, 0), top_coupling[entry])
        product = term if product is None else product + term
    top_local = pair(quarters(product), 0)

    def step(turn, carry):
        for inner in range(2):
            group = turn * 2 + inner
            product = dot_nt(top_local, top_split[group])
            for entry in range(entries):
                index = mid_list[group, entry]
                where = jnp.where(index >= 0, index - first, groups)
                product = product + dot(table[where], mid_coupling[group * entries + entry])
            total[group] = quarters(product)
        return carry

    lax.fori_loop(0, groups // 2, step, 0)


def product_body(
    members, near, again, near_list, noise, low, own, high, blocks, operator, total, top_split, *rest
):
    if again:
        out, wide, top, table = rest
    else:
        out, table = rest
    leaves, probe_count, points = out.shape
    rank = total.shape[2]
    groups = total.shape[0]
    skip = low.shape[1] - probe_count
    first = (lax.axis_index("leaf") * lax.axis_size("sub") + lax.axis_index("sub") - 1) * leaves

    def fill(leaf, carry):
        table[leaf] = low[leaf, skip:]
        table[leaves + leaf] = own[leaf]
        table[2 * leaves + leaf] = high[leaf, skip:]
        return carry

    lax.fori_loop(0, leaves, fill, 0, unroll=8)

    def column(leaf, entry):
        index = near_list[leaf, entry]
        return jnp.where(index >= 0, index - first, leaves)

    def step(group, carry):
        local = pair(total[group], 1)
        upper, lower = local[:, :rank], local[:, rank:]
        far = jnp.concatenate([upper, upper, lower, jnp.zeros_like(lower)], axis=1)
        for member in range(members):
            leaf = group * members + member
            gathered = [table[column(leaf, entry)] for entry in range(near)] + [far]
            near_weights = blocks[pl.ds(leaf * near, near)].reshape(near * points, points)
            weights = jnp.concatenate([near_weights, operator[leaf], operator[leaf]], axis=0)
            value = dot(jnp.concatenate(gathered, axis=1), weights)
            value = value + noise[0] * own[leaf].astype(F32)
            out[leaf] = value.astype(BF16)
            if again:
                wide[leaf] = value.astype(BF16)
        if again:
            coef = up_group(lambda leaf: out[leaf], operator, group, members)
            wide[leaves + group] = pair(coef, 1)
            carry = carry + up_top(coef, top_split[group])
        return carry

    result = lax.fori_loop(0, groups, step, jnp.zeros((probe_count, rank), F32))
    if again:
        top[...] = jnp.broadcast_to(pair(result, 1), top.shape)


def neighbours(block):
    count = lax.axis_size(AXES)
    forward = [(i, i + 1) for i in range(count - 1)]
    backward = [(target, source) for source, target in forward]
    return lax.ppermute(block, AXES, forward), lax.ppermute(block, AXES, backward)


def top_steps(partial):
    def exchange(value, axis, step):
        size = lax.axis_size(axis)
        other = lax.ppermute(value, axis, [(i, i ^ step) for i in range(size)])
        return other

    partial = partial + exchange(partial, "sub", 1)
    blocks = partial[None]
    step = 1
    while step < lax.axis_size("leaf"):
        blocks = jnp.concatenate([blocks, exchange(blocks, "leaf", step)], axis=0)
        step *= 2
    step = 2
    while step < lax.axis_size("sub"):
        blocks = blocks + exchange(blocks, "sub", step)
        step *= 2
    return blocks


def work_list(near_list, position, leaves):
    flat = near_list.reshape(-1)
    count = flat.shape[0]
    column = flat - position * leaves
    own = (column >= 0) & (column < leaves)
    kind = jnp.where(flat < 0, 2, jnp.where(own, 0, 1))
    column = jnp.where(own, column, jnp.where(column < 0, column + leaves, column))
    item = jnp.arange(count, dtype=jnp.int32)
    code = item + (jnp.where(flat < 0, 0, column) << 16)
    key = kind * count + item
    place = jnp.sum((key[:, None] > key[None, :]).astype(jnp.int32), axis=1)
    index = jnp.arange(count + 2, dtype=jnp.int32)[None, :]
    entry = jnp.where(
        index < count,
        jnp.where(place[:, None] == index, code[:, None], 0),
        (kind[:, None] == index - count).astype(jnp.int32),
    )
    return jnp.sum(entry, axis=0)


def on_device(
    points,
    probes,
    leaf_basis,
    mid_transfer,
    top_transfer,
    mid_skeleton,
    top_skeleton,
    near_list,
    mid_list,
    top_list,
    inv_scale,
    amplitude,
    noise_var,
):
    leaves, feat, size = points.shape
    groups, _, rank = mid_skeleton.shape
    probe_count = probes.shape[1]
    members = leaves // groups
    near = near_list.shape[1]
    entries = mid_list.shape[1]
    sds = jax.ShapeDtypeStruct
    slots = leaves * near
    devices = lax.axis_size(AXES)

    operator, mid, top, top_split = call(
        functools.partial(prepare_body, members),
        [
            sds((leaves, 2 * rank, size), BF16),
            sds((leaves + groups, 2 * feat + probe_count, size), BF16),
            sds((probe_count, rank), F32),
            sds((groups, 2 * rank, rank), BF16),
        ],
        [SMEM] + [HBM] * 6,
        scratch=[
            pltpu.VMEM(points.shape, F32),
            pltpu.VMEM(leaf_basis.shape, BF16),
            pltpu.VMEM(mid_transfer.shape, F32),
            pltpu.VMEM(top_transfer.shape, F32),
            pltpu.VMEM(mid_skeleton.shape, F32),
            pltpu.SemaphoreType.DMA((3, groups)),
            pltpu.SemaphoreType.DMA((3,)),
        ],
        micros=5,
        limit=67043328,
    )(inv_scale, points, probes, leaf_basis, mid_transfer, top_transfer, mid_skeleton)
    position = lax.axis_index("leaf") * lax.axis_size("sub") + lax.axis_index("sub")
    items = work_list(near_list, position, leaves)

    blocks_shape = sds((slots, size, size), BF16)
    for part in range(PARTS):
        body = functools.partial(local_body, near, part, PARTS)
        if part == 0:
            blocks, right, left = call(
                body,
                [
                    blocks_shape,
                    sds((leaves, 8 * feat, size), BF16),
                    sds((leaves, size, 8 * feat), BF16),
                ],
                [SMEM] * 3 + [VMEM],
                micros=4,
            )(items, amplitude, inv_scale, points)
        else:
            blocks = call(
                body, [blocks_shape], [SMEM] * 3 + [VMEM] * 3, aliases={5: 0}, micros=3
            )(items, amplitude, inv_scale, right, left, blocks)[0]

    vector = probes
    results = []
    for turn in range(MATVECS):
        again = turn + 1 < MATVECS
        low, high = neighbours(mid)
        if turn == 0:
            tops = top_steps(top)
        else:
            tops = lax.all_to_all(top, AXES, 0, 0, tiled=True)
        if turn == 0:
            blocks = call(
                functools.partial(halo_body, near),
                [blocks_shape],
                [SMEM] * 2 + [VMEM] * 4,
                scratch=[pltpu.VMEM((2 * leaves, size, 8 * feat), BF16)],
                aliases={5: 0},
                micros=9,
            )(items, amplitude, low, high, right, blocks)[0]
            mid_coupling, top_coupling = call(
                functools.partial(skeleton_body, entries),
                [
                    sds((groups * entries, rank, 2 * rank), BF16),
                    sds((top_list.shape[1], rank, 2 * rank), BF16),
                ],
                [SMEM] * 4 + [VMEM] * 4,
                scratch=[
                    pltpu.VMEM((3 * groups, rank, 8 * feat), BF16),
                    pltpu.VMEM((groups, 8 * feat, rank), BF16),
                ],
                micros=4,
            )(mid_list, top_list, amplitude, inv_scale, mid, low, high, top_skeleton)
        middle = call(
            functools.partial(middle_body, entries, turn == 0),
            [sds((groups, probe_count, rank), F32)],
            [SMEM] * 2 + [VMEM] * 7,
            scratch=[pltpu.VMEM((3 * groups, 2 * probe_count, rank), BF16)],
            micros=2,
        )(
            mid_list, top_list, mid, low, high, tops,
            mid_coupling, top_coupling, top_split,
        )[0]
        outs = [sds(vector.shape, BF16)]
        if again:
            outs += [
                sds((leaves + groups, probe_count, 2 * rank), BF16),
                sds((devices, probe_count, 2 * rank), BF16),
            ]
        values = call(
            functools.partial(product_body, members, near, again),
            outs,
            [SMEM] * 2 + [VMEM] * 7,
            scratch=[pltpu.VMEM((3 * leaves, probe_count, size), BF16)],
            micros=8,
        )(near_list, noise_var, low, vector, high, blocks, operator, middle, top_split)
        vector = values[0]
        results.append(vector)
        if again:
            mid, top = values[1], values[2]
    return (results[0], results[1])


def solution(mesh):
    whole = P(AXES, None, None)
    in_specs = (
        whole, whole, whole, whole, whole, whole,
        P(), P(AXES, None), P(AXES, None), P("leaf", None), P(), P(), P(),
    )

    return jax.shard_map(
        on_device, mesh=mesh, in_specs=in_specs, out_specs=(whole, whole), check_vma=False
    )
```
